256 devices in a mesh: bx: 32 (over z, y), by: 8 (over x, core).
Axes of the slice: x: 4, y: 4, z: 8, core: 2. Of those that a mesh axis runs over, the one named last changes fastest.
Arguments:
- source: bfloat16 [32, 8, 2, 128, 1024], P('bx', 'by'), may hold values from -6 to 6
- start_tick: int32 [32, 8], P('bx', 'by'), may hold values from 0 to 3, as said below
- op_x: bfloat16 [32, 8, 2, 1024, 1024], P('bx', 'by'), may hold values from -0.09375 to 0.09375
- op_y: bfloat16 [32, 8, 2, 1024, 1024], P('bx', 'by'), may hold values from -0.09375 to 0.09375
Outputs:
- upgoing: float32 [8, 128, 2, 32, 1024], P('by', 'bx')
The draws below stay inside these ranges and needn't reach their ends.
Inputs may be any that keep to these rules, and one draw needn't show every extreme that they name: `start_tick`: both 0 and 3 occur in every draw.
All inputs are finite; a program needn't handle non-finite values.
Results may differ from the reference program's by a relative error of at most 0.012.
Values may be sent and summed in bfloat16 or wider, within the bound.
No kernel may reach another device: no remote copies, remote signals or barrier semaphores. Data moves between devices by JAX's collectives and lax.ppermute only.
A program may use at most 64 MiB of HBM per device.

```python
import math
import jax
import jax.numpy as jnp
from jax import lax

F = 1024
SHOTS = 128
TICKS = 4
GRID_X = 32
GRID_Y = 8


def draw_start_tick(key, part):
    values = jax.random.randint(key, (GRID_X, GRID_Y), 0, TICKS)
    values = values.at[0, 0].set(0).at[GRID_X - 1, GRID_Y - 1].set(TICKS - 1)
    return values.astype(jnp.int32)


def level_of(own_key, shape, shards, smallest, top_value):
    gain = 1.0
    for dim, blocks in shards:
        draws = jax.random.uniform(jax.random.fold_in(jax.random.fold_in(own_key, 6), dim), (blocks,), jnp.float32, smallest / len(shards), top_value / len(shards))
        gain = gain * jnp.repeat(jnp.exp(draws), shape[dim] // blocks).reshape((-1,) + (1,) * (len(shape) - 1 - dim))
    return gain


def bell_draw(rng, dims, spread, limit, shards=(), kind=jnp.bfloat16):
    values = jax.random.normal(rng, dims, jnp.float32) * spread
    if len(shards) > 0:
        values = level_of(rng, dims, shards, -0.22, 0.18) * values
    return jnp.clip(values, min=-limit, max=limit).astype(kind)


def setup_inputs(seed: int = 0) -> dict:
    streams_of = jax.random.split(jax.random.key(seed), 5)
    source = bell_draw(streams_of[0], (GRID_X, GRID_Y, 2, SHOTS, F), 1.0, 6.0, ((0, 32), (1, 8)))
    start_tick = draw_start_tick(jax.random.fold_in(streams_of[4], 71), 0)
    op_x = bell_draw(streams_of[2], (GRID_X, GRID_Y, 2, F, F), (4 * F) ** -0.5, 0.09375, ((0, 32), (1, 8)))
    op_y = bell_draw(streams_of[3], (GRID_X, GRID_Y, 2, F, F), (4 * F) ** -0.5, 0.09375, ((0, 32), (1, 8)))
    return {"source": source, "start_tick": start_tick, "op_x": op_x, "op_y": op_y}


def dft_tables(length):
    indices = jnp.arange(length, dtype=jnp.int32)
    products = indices[:, None] * indices[None, :] % length
    angles = products.astype(jnp.float32) * (2.0 * math.pi / length)
    return (jnp.cos(angles).astype(jnp.bfloat16), jnp.sin(angles).astype(jnp.bfloat16))

def complex_apply(traces, operator):

    def one_row(pair):
        trace_row = pair[0].astype(jnp.float32)
        operator_row = pair[1].astype(jnp.float32)
        with_real = jnp.einsum('jcsf,jfk->jcsk', trace_row, operator_row[:, 0])
        with_imag = jnp.einsum('jcsf,jfk->jcsk', trace_row, operator_row[:, 1])
        real_out = with_real[:, 0] - with_imag[:, 1]
        imag_out = with_imag[:, 0] + with_real[:, 1]
        return jnp.stack([real_out, imag_out], axis=1)
    return lax.map(one_row, (traces, operator))

def shift_down(values, axis):
    widths = [(0, 0)] * values.ndim
    widths[axis] = (1, 0)
    kept = lax.slice_in_dim(values, 0, values.shape[axis] - 1, axis=axis)
    return jnp.pad(kept, widths)

def shift_up(values, axis):
    widths = [(0, 0)] * values.ndim
    widths[axis] = (0, 1)
    kept = lax.slice_in_dim(values, 1, values.shape[axis], axis=axis)
    return jnp.pad(kept, widths)

def reference(source, start_tick, op_x, op_y):
    east_out = jnp.zeros(source.shape, jnp.bfloat16)
    north_out = jnp.zeros(source.shape, jnp.bfloat16)
    source32 = source.astype(jnp.float32)
    for tick in range(TICKS):
        from_west = shift_down(east_out, 0).astype(jnp.float32)
        from_south = shift_down(north_out, 1).astype(jnp.float32)
        active = (start_tick <= tick).astype(jnp.float32)[:, :, None, None, None]
        incident = (from_west + from_south + active * source32).astype(jnp.bfloat16)
        east_out = complex_apply(incident, op_x).astype(jnp.bfloat16)
        north_out = complex_apply(incident, op_y).astype(jnp.bfloat16)
    mismatch = (shift_down(east_out, 0).astype(jnp.float32) + shift_down(north_out, 1).astype(jnp.float32) - shift_up(east_out, 0).astype(jnp.float32) - shift_up(north_out, 1).astype(jnp.float32)).astype(jnp.bfloat16)
    reflected = complex_apply(mismatch, op_x).astype(jnp.bfloat16)
    cos_line, sin_line = dft_tables(F)
    refl32 = reflected.astype(jnp.float32)
    cos32 = cos_line.astype(jnp.float32)
    sin32 = sin_line.astype(jnp.float32)
    spec_real = jnp.einsum('ijsf,fk->ijsk', refl32[:, :, 0], cos32) + jnp.einsum('ijsf,fk->ijsk', refl32[:, :, 1], sin32)
    spec_imag = jnp.einsum('ijsf,fk->ijsk', refl32[:, :, 1], cos32) - jnp.einsum('ijsf,fk->ijsk', refl32[:, :, 0], sin32)
    spectrum_real = spec_real.astype(jnp.bfloat16).astype(jnp.float32)
    spectrum_imag = spec_imag.astype(jnp.bfloat16).astype(jnp.float32)
    cos_grid, sin_grid = dft_tables(GRID_X)
    cosg = cos_grid.astype(jnp.float32)
    sing = sin_grid.astype(jnp.float32)
    out_real = jnp.einsum('ijsk,iq->jsqk', spectrum_real, cosg) + jnp.einsum('ijsk,iq->jsqk', spectrum_imag, sing)
    out_imag = jnp.einsum('ijsk,iq->jsqk', spectrum_imag, cosg) - jnp.einsum('ijsk,iq->jsqk', spectrum_real, sing)
    wave_index = jnp.arange(GRID_X, dtype=jnp.int32)
    signed = jnp.where(wave_index < GRID_X // 2, wave_index, wave_index - GRID_X).astype(jnp.float32)
    weights = 0.5 * (1.0 + signed / jnp.sqrt(signed * signed + 1.0))
    return jnp.stack([out_real, out_imag], axis=2) * weights[None, None, None, :, None]
```

```python
import math

import jax
import jax.numpy as jnp
import numpy as np
from jax import lax
from jax.sharding import PartitionSpec as P

F = 1024
TICKS = 4
SHOTS = 128


def shift(value, axis, by):
    n = lax.axis_size(axis)
    return lax.ppermute(value, axis, [(i, (i + by) % n) for i in range(n)])


def paired(block):
    re, im = block[0], block[1]
    return jnp.concatenate(
        [jnp.concatenate([re, -im], axis=1), jnp.concatenate([im, re], axis=1)], axis=0
    )


def apply(pair, operator):
    out = jnp.dot(pair, operator, preferred_element_type=jnp.float32)
    return out.astype(jnp.bfloat16)


def line_table(tie):
    k = jnp.arange(F, dtype=jnp.int32)[None, :] + tie
    a = jnp.arange(32, dtype=jnp.int32)[:, None]
    coarse = (a * 32 * k % F).astype(jnp.float32) * (2.0 * math.pi / F)
    fine = (a * k % F).astype(jnp.float32) * (2.0 * math.pi / F)
    ca, sa, cb, sb = lax.optimization_barrier(
        (jnp.cos(coarse), jnp.sin(coarse), jnp.cos(fine), jnp.sin(fine))
    )
    cos = ca[:, None, :] * cb[None, :, :] - sa[:, None, :] * sb[None, :, :]
    sin = sa[:, None, :] * cb[None, :, :] + ca[:, None, :] * sb[None, :, :]
    return jnp.stack([cos, sin]).astype(jnp.bfloat16).reshape(2 * F, F)


def line_weights(blocks, owned):
    u = 2.0 * np.pi * (np.outer(np.arange(blocks), np.arange(blocks)) % blocks) / blocks
    cos = np.cos(u).astype(np.float32)
    sin = np.sin(u).astype(np.float32)
    w = np.zeros((owned, 2, blocks, blocks, 2, owned), np.float32)
    for s in range(owned):
        w[s, 0, :, :, 0, s] = cos.T
        w[s, 0, :, :, 1, s] = sin.T
        w[s, 1, :, :, 1, s] = cos.T
        w[s, 1, :, :, 0, s] = -sin.T
    m = np.where(np.arange(blocks) < blocks // 2, np.arange(blocks), np.arange(blocks) - blocks)
    g = 0.5 * (1.0 + m / np.sqrt(m * m + 1.0))
    rows = np.broadcast_to(g[None, None, :], (owned, 2, blocks)).reshape(-1, 1)
    n = owned * 2 * blocks
    return jnp.asarray(w.reshape(n, n), jnp.bfloat16), jnp.asarray(rows, jnp.float32)


def shards(source, start_tick, op_x, op_y):
    nx, ny = lax.axis_size("bx"), lax.axis_size("by")
    i, j = lax.axis_index("bx"), lax.axis_index("by")
    src = source[0, 0].astype(jnp.float32)
    x_op = op_x.reshape(2 * F, F)
    y_op = op_y.reshape(2 * F, F)
    first = start_tick[0, 0]

    def inside(flag, value):
        return jnp.where(flag, value.astype(jnp.float32), 0.0)

    east = north = None
    table = None
    for tick in range(TICKS):
        own = jnp.where(first <= tick, src, 0.0)
        if tick == 0:
            incident = own.astype(jnp.bfloat16)
        else:
            incident = (inside(i > 0, from_west) + inside(j > 0, from_south) + own).astype(jnp.bfloat16)
        pair = lax.optimization_barrier(paired(incident))
        east = apply(pair, x_op).reshape(2, SHOTS, F)
        from_west = shift(east, "bx", 1)
        if tick == TICKS - 1:
            from_east = shift(east, "bx", -1)
        north = apply(pair, y_op).reshape(2, SHOTS, F)
        from_south = shift(north, "by", 1)
        if tick == TICKS - 1:
            from_north = shift(north, "by", -1)
        if tick == 1:
            tie = jnp.minimum(first, 0) * (pair[0, 0] > 1e30).astype(jnp.int32)
            table = line_table(tie)
    mismatch = (
        inside(i > 0, from_west)
        + inside(j > 0, from_south)
        - inside(i < nx - 1, from_east)
        - inside(j < ny - 1, from_north)
    ).astype(jnp.bfloat16)
    reflected = apply(lax.optimization_barrier(paired(mismatch)), x_op).reshape(2, SHOTS, F)
    re, im = reflected[0], reflected[1]
    turned = jnp.concatenate(
        [jnp.concatenate([re, im], axis=1), jnp.concatenate([im, -re], axis=1)], axis=0
    )
    spectrum = apply(lax.optimization_barrier(turned), table)
    owned = SHOTS // nx
    pieces = spectrum.reshape(2, nx, owned, F).transpose(1, 0, 2, 3).reshape(nx, 2 * owned, F)
    regrouped = lax.all_to_all(pieces, "bx", split_axis=0, concat_axis=0, tiled=True)
    weights, gain = line_weights(nx, owned)
    up = jnp.dot(weights, regrouped.reshape(nx * 2 * owned, F), preferred_element_type=jnp.float32)
    return (up * gain).reshape(1, owned, 2, nx, F)


def solution(mesh):
    placed = (
        P("bx", "by", None, None, None),
        P("bx", "by"),
        P("bx", "by", None, None, None),
        P("bx", "by", None, None, None),
    )
    return jax.shard_map(
        shards,
        mesh=mesh,
        in_specs=placed,
        out_specs=P("by", "bx", None, None, None),
        check_vma=False,
    )
```

```python
import functools

import jax
import jax.numpy as jnp
import numpy as np
from jax import lax
from jax.experimental import pallas as pl
from jax.experimental.pallas import tpu as pltpu
from jax.sharding import PartitionSpec as P


F = 1024
TICKS = 4
SHOTS = 128
CUTS = (0, 64, 128)
CHUNKS = len(CUTS) - 1
STEP = 512
BF16 = jnp.bfloat16
F32 = jnp.float32
MIB = 1 << 20


def shift(value, axis, by):
    n = lax.axis_size(axis)
    return lax.ppermute(value, axis, [(i, (i + by) % n) for i in range(n)])


def vmem():
    return pl.BlockSpec(memory_space=pltpu.VMEM)


def smem():
    return pl.BlockSpec(memory_space=pltpu.SMEM)


def anywhere():
    return pl.BlockSpec(memory_space=pl.ANY)


def call(kernel, outs, specs, args, flops, scratch=(), limit=12):
    return pl.pallas_call(
        kernel,
        out_shape=[jax.ShapeDtypeStruct(shape, kind) for shape, kind in outs],
        in_specs=specs,
        out_specs=[vmem() for _ in outs],
        scratch_shapes=list(scratch),
        compiler_params=pltpu.CompilerParams(vmem_limit_bytes=limit * MIB),
        cost_estimate=pl.CostEstimate(flops=flops, bytes_accessed=MIB, transcendentals=0),
    )(*args)


def product(pair, operator, out):
    w = out.shape[1]
    for c in range(0, F, STEP):
        total = jnp.dot(pair[:, :F], operator[0, :, c : c + STEP], preferred_element_type=F32)
        total += jnp.dot(pair[:, F:], operator[1, :, c : c + STEP], preferred_element_type=F32)
        out[0, :, c : c + STEP] = total[:w].astype(BF16)
        out[1, :, c : c + STEP] = total[w:].astype(BF16)


def fill(pair, re, im):
    w = re.shape[0]
    pair[:w, :F] = re.astype(BF16)
    pair[:w, F:] = (-im).astype(BF16)
    pair[w:, :F] = im.astype(BF16)
    pair[w:, F:] = re.astype(BF16)


def wide(flag, value):
    return jnp.where(flag != 0, value.astype(F32), 0.0)


def east_kernel(tick, lo, hi, flags, *refs):
    if tick == 0:
        src, op, _, out, pair = refs
        parts = [wide(flags[0] <= tick, src[c, lo:hi]) for c in range(2)]
    else:
        src, west, south, op, _, out, pair = refs
        parts = [
            wide(flags[1], west[c]) + wide(flags[2], south[c]) + wide(flags[0] <= tick, src[c, lo:hi])
            for c in range(2)
        ]
    fill(pair, *parts)
    product(pair, op, out)


def north_kernel(pair, op, out):
    product(pair, op, out)


def table_kernel(coarse, fine, _, out):
    for a in range(32):
        ca, sa = coarse[0, a : a + 1, :], coarse[1, a : a + 1, :]
        cb, sb = fine[0], fine[1]
        out[0, 32 * a : 32 * a + 32, :] = (ca * cb - sa * sb).astype(BF16)
        out[1, 32 * a : 32 * a + 32, :] = (sa * cb + ca * sb).astype(BF16)


def mirror_kernel(flags, west, south, east, north, op, table, _, out, pair, refl):
    parts = [
        wide(flags[1], west[c])
        + wide(flags[2], south[c])
        - wide(flags[3], east[c])
        - wide(flags[4], north[c])
        for c in range(2)
    ]
    fill(pair, *parts)
    product(pair, op, refl)
    w = refl.shape[1]
    re, im = refl[0], refl[1]
    pair[:w, :F] = re
    pair[:w, F:] = im
    pair[w:, :F] = im
    pair[w:, F:] = -re
    product(pair, table, refl)
    r = lax.broadcasted_iota(jnp.int32, (2 * w, 2 * w), 0)
    k = lax.broadcasted_iota(jnp.int32, (2 * w, 2 * w), 1)
    from_row = (r % 8) // 4 * w + r // 8 * 4 + r % 4
    pick = jnp.where(k == from_row, 1.0, 0.0).astype(BF16)
    for c in range(0, F, STEP):
        rows = jnp.concatenate([refl[0, :, c : c + STEP], refl[1, :, c : c + STEP]], axis=0)
        moved = jnp.dot(pick, rows, preferred_element_type=F32).astype(BF16)
        out[:, :, c : c + STEP] = moved.reshape(w // 4, 8, STEP)


def last_kernel(weights, gain, got, out):
    out[...] = jnp.dot(weights[...], got[...], preferred_element_type=F32) * gain[...]


def line_parts():
    k = np.arange(F, dtype=np.int64)[None, :]
    a = np.arange(32, dtype=np.int64)[:, None]
    coarse = 2.0 * np.pi / F * (a * 32 * k % F)
    fine = 2.0 * np.pi / F * (a * k % F)
    pack = lambda t: jnp.asarray(np.stack([np.cos(t), np.sin(t)]).astype(np.float32))
    return pack(coarse), pack(fine)


def line_weights(blocks, owned):
    u = 2.0 * np.pi * (np.outer(np.arange(blocks), np.arange(blocks)) % blocks) / blocks
    cos = np.cos(u).astype(np.float32)
    sin = np.sin(u).astype(np.float32)
    w = np.zeros((owned, 2, blocks, blocks, 2, owned), np.float32)
    for s in range(owned):
        w[s, 0, :, :, 0, s] = cos.T
        w[s, 0, :, :, 1, s] = sin.T
        w[s, 1, :, :, 1, s] = cos.T
        w[s, 1, :, :, 0, s] = -sin.T
    m = np.where(np.arange(blocks) < blocks // 2, np.arange(blocks), np.arange(blocks) - blocks)
    g = 0.5 * (1.0 + m / np.sqrt(m * m + 1.0))
    n = owned * 2 * blocks
    gain = np.broadcast_to(g[None, None, :, None], (owned, 2, blocks, F)).reshape(n, F)[:, :1]
    return jnp.asarray(w.reshape(n, n), BF16), jnp.asarray(gain, F32)


def shards(source, start_tick, op_x, op_y):
    nx, ny = lax.axis_size("bx"), lax.axis_size("by")
    i, j = lax.axis_index("bx"), lax.axis_index("by")
    src, x_op, y_op = source[0, 0], op_x[0, 0], op_y[0, 0]
    flags = jnp.stack(
        [
            start_tick[0, 0],
            (i > 0).astype(jnp.int32),
            (j > 0).astype(jnp.int32),
            (i < nx - 1).astype(jnp.int32),
            (j < ny - 1).astype(jnp.int32),
        ]
    )
    coarse, fine = line_parts()
    west, south, ahead, above = ([None] * CHUNKS for _ in range(4))
    last = start_tick
    table = None
    sizes = []
    for lo, hi in zip(CUTS[:-1], CUTS[1:]):
        w = hi - lo
        sizes.append((w, ((2, w, F), BF16), ((2 * w, 2 * F), BF16), 2 * (2 * w) * (2 * F) * F))
    for tick in range(TICKS):
        for c in range(CHUNKS):
            w, trace, paired, flops = sizes[c]
            body = functools.partial(east_kernel, tick, CUTS[c], CUTS[c + 1])
            if tick == 0:
                specs = [smem(), vmem(), vmem(), anywhere()]
                args = [flags, src, x_op, last]
            else:
                specs = [smem(), vmem(), vmem(), vmem(), vmem(), anywhere()]
                args = [flags, src, west[c], south[c], x_op, last]
            east, pair = call(body, [trace, paired], specs, args, flops)
            west[c] = shift(east, "bx", 1)
            if tick == TICKS - 1:
                ahead[c] = shift(east, "bx", -1)
            (north,) = call(north_kernel, [trace], [vmem(), vmem()], [pair, y_op], flops)
            south[c] = shift(north, "by", 1)
            if tick == TICKS - 1:
                above[c] = shift(north, "by", -1)
            last = north
        if tick == 1:
            (table,) = call(
                table_kernel, [((2, F, F), BF16)], [vmem(), vmem(), anywhere()], [coarse, fine, last], flops
            )
            last = table
    owned = SHOTS // nx
    spectra = []
    for c in range(CHUNKS):
        w, trace, paired, flops = sizes[c]
        (piece,) = call(
            mirror_kernel,
            [((w // owned, 2 * owned, F), BF16)],
            [smem()] + [vmem()] * 6 + [anywhere()],
            [flags, west[c], south[c], ahead[c], above[c], x_op, table, last],
            2 * flops,
            [pltpu.VMEM(paired[0], BF16), pltpu.VMEM(trace[0], BF16)],
        )
        spectra.append(piece)
        last = piece
    pieces = jnp.concatenate(spectra, axis=0)
    regrouped = lax.all_to_all(pieces, "bx", split_axis=0, concat_axis=0, tiled=True)
    weights, gain = line_weights(nx, owned)
    (up,) = call(
        last_kernel,
        [((nx * 2 * owned, F), F32)],
        [vmem()] * 3,
        [weights, gain, regrouped.reshape(nx * 2 * owned, F)],
        1 << 27,
    )
    return up.reshape(1, owned, 2, nx, F)


def solution(mesh):
    placed = (
        P("bx", "by", None, None, None),
        P("bx", "by"),
        P("bx", "by", None, None, None),
        P("bx", "by", None, None, None),
    )

    return jax.shard_map(
        shards,
        mesh=mesh,
        in_specs=placed,
        out_specs=P("by", "bx", None, None, None),
        check_vma=False,
    )
```

```python
import functools

import jax
import jax.numpy as jnp
import numpy as np
from jax import lax
from jax.experimental import pallas as pl
from jax.experimental.pallas import tpu as pltpu
from jax.sharding import PartitionSpec as P


F = 1024
TICKS = 4
SHOTS = 128
CUTS = (0, 64, 128)
CHUNKS = len(CUTS) - 1
STEP = 512
TABLE = 1
EAST_FIRST = False
BF16 = jnp.bfloat16
F32 = jnp.float32
MIB = 1 << 20


def shift(value, axis, by):
    n = lax.axis_size(axis)
    return lax.ppermute(value, axis, [(i, (i + by) % n) for i in range(n)])


def swap(value, axis, odd):
    n = lax.axis_size(axis)
    partner = [k ^ 1 if not odd else min(max(((k + 1) ^ 1) - 1, 0), n - 1) for k in range(n)]
    partner = [k if partner[p] != k else p for k, p in enumerate(partner)]
    return lax.ppermute(value, axis, list(enumerate(partner)))


def vmem():
    return pl.BlockSpec(memory_space=pltpu.VMEM)


def anywhere():
    return pl.BlockSpec(memory_space=pl.ANY)


def call(kernel, outs, specs, args, flops, scratch=(), limit=12):
    return pl.pallas_call(
        kernel,
        out_shape=[jax.ShapeDtypeStruct(shape, kind) for shape, kind in outs],
        in_specs=specs,
        out_specs=[vmem() for _ in outs],
        scratch_shapes=list(scratch),
        compiler_params=pltpu.CompilerParams(vmem_limit_bytes=limit * MIB),
        cost_estimate=pl.CostEstimate(flops=flops, bytes_accessed=MIB, transcendentals=0),
    )(*args)


def combine(real, imag, out, lo, hi):
    w = out.shape[1]
    out[0, :, lo:hi] = (real[:w] - imag[w:]).astype(BF16)
    out[1, :, lo:hi] = (imag[:w] + real[w:]).astype(BF16)


def product(pair, operator, out):
    for c in range(0, F, STEP):
        real = jnp.dot(pair[...], operator[0, :, c : c + STEP], preferred_element_type=F32)
        imag = jnp.dot(pair[...], operator[1, :, c : c + STEP], preferred_element_type=F32)
        combine(real, imag, out, c, c + STEP)


def fill(pair, rows):
    w = pair.shape[0] // 2
    for part in range(2):
        for r in range(0, w, 16):
            pair[part * w + r : part * w + r + 16] = rows(part, r).astype(BF16)


FROM_WEST, FROM_SOUTH, FAR_X, FAR_Y, SIGN_X, SIGN_Y = range(TICKS, TICKS + 6)


def row(masks, k):
    return masks[k : k + 1]


def open_kernel(masks, src, *pairs):
    for lo, pair in zip(CUTS, pairs):
        fill(pair, lambda c, r: row(masks, 0) * src[c, lo + r : lo + r + 16].astype(F32))


def east_kernel(tick, lo, masks, src, west, south, op, *rest):
    out, pair = rest[-2:]

    def rows(c, r):
        at = pl.ds(r, 16)
        return (
            row(masks, FROM_WEST) * west[c, at].astype(F32)
            + row(masks, FROM_SOUTH) * south[c, at].astype(F32)
            + row(masks, tick) * src[c, lo + r : lo + r + 16].astype(F32)
        )

    fill(pair, rows)
    product(pair, op, out)


def product_kernel(pair, op, *rest):
    product(pair, op, rest[-1])


def table_kernel(coarse, fine, _, out):
    for a in range(32):
        ca, sa = coarse[0, a : a + 1, :], coarse[1, a : a + 1, :]
        cb, sb = fine[0], fine[1]
        out[0, 32 * a : 32 * a + 32, :] = (ca * cb - sa * sb).astype(BF16)
        out[1, 32 * a : 32 * a + 32, :] = (sa * cb + ca * sb).astype(BF16)


def mirror_kernel(masks, east1, east2, north1, north2, op, table, _, out, pair, refl):
    def rows(c, r):
        at = pl.ds(r, 16)
        along_x = east1[c, at].astype(F32) - row(masks, FAR_X) * east2[c, at].astype(F32)
        along_y = north1[c, at].astype(F32) - row(masks, FAR_Y) * north2[c, at].astype(F32)
        return row(masks, SIGN_X) * along_x + row(masks, SIGN_Y) * along_y

    fill(pair, rows)
    product(pair, op, refl)
    w = refl.shape[1]
    pair[:w] = refl[0]
    pair[w:] = refl[1]
    for c in range(0, F, STEP):
        cos = jnp.dot(pair[...], table[0, :, c : c + STEP], preferred_element_type=F32)
        sin = jnp.dot(pair[...], table[1, :, c : c + STEP], preferred_element_type=F32)
        combine(cos, -sin, refl, c, c + STEP)
    r = lax.broadcasted_iota(jnp.int32, (2 * w, 2 * w), 0)
    k = lax.broadcasted_iota(jnp.int32, (2 * w, 2 * w), 1)
    from_row = (r % 8) // 4 * w + r // 8 * 4 + r % 4
    pick = jnp.where(k == from_row, 1.0, 0.0).astype(BF16)
    for c in range(0, F, STEP):
        rows = jnp.concatenate([refl[0, :, c : c + STEP], refl[1, :, c : c + STEP]], axis=0)
        moved = jnp.dot(pick, rows, preferred_element_type=F32).astype(BF16)
        out[:, :, c : c + STEP] = moved.reshape(w // 4, 8, STEP)


def last_kernel(weights, gain, got, out):
    out[...] = jnp.dot(weights[...], got[...], preferred_element_type=F32) * gain[...]


def line_parts():
    k = np.arange(F, dtype=np.int64)[None, :]
    a = np.arange(32, dtype=np.int64)[:, None]
    coarse = 2.0 * np.pi / F * (a * 32 * k % F)
    fine = 2.0 * np.pi / F * (a * k % F)
    pack = lambda t: jnp.asarray(np.stack([np.cos(t), np.sin(t)]).astype(np.float32))
    return pack(coarse), pack(fine)


def line_weights(blocks, owned):
    u = 2.0 * np.pi * (np.outer(np.arange(blocks), np.arange(blocks)) % blocks) / blocks
    cos = np.cos(u).astype(np.float32)
    sin = np.sin(u).astype(np.float32)
    w = np.zeros((owned, 2, blocks, blocks, 2, owned), np.float32)
    for s in range(owned):
        w[s, 0, :, :, 0, s] = cos.T
        w[s, 0, :, :, 1, s] = sin.T
        w[s, 1, :, :, 1, s] = cos.T
        w[s, 1, :, :, 0, s] = -sin.T
    m = np.where(np.arange(blocks) < blocks // 2, np.arange(blocks), np.arange(blocks) - blocks)
    g = 0.5 * (1.0 + m / np.sqrt(m * m + 1.0))
    n = owned * 2 * blocks
    gain = np.broadcast_to(g[None, None, :, None], (owned, 2, blocks, F)).reshape(n, F)[:, :1]
    return jnp.asarray(w.reshape(n, n), BF16), jnp.asarray(gain, F32)


def shards(source, start_tick, op_x, op_y):
    nx, ny = lax.axis_size("bx"), lax.axis_size("by")
    i, j = lax.axis_index("bx"), lax.axis_index("by")
    src, x_op, y_op = source[0, 0], op_x[0, 0], op_y[0, 0]
    first = start_tick[0, 0]
    flags = jnp.stack(
        [(first <= tick).astype(jnp.int32) for tick in range(TICKS)]
        + [
            (i > 0).astype(jnp.int32),
            (j > 0).astype(jnp.int32),
            ((i > 0) & (i < nx - 1)).astype(jnp.int32),
            ((j > 0) & (j < ny - 1)).astype(jnp.int32),
            2 * (i & 1) - 1,
            2 * (j & 1) - 1,
        ]
        + [jnp.int32(0)] * 6
    )
    masks = jnp.broadcast_to(flags.astype(F32)[:, None], (16, F))
    coarse, fine = line_parts()
    west, south, ahead, above = ([None] * CHUNKS for _ in range(4))
    last = start_tick
    table = None
    sizes = []
    for lo, hi in zip(CUTS[:-1], CUTS[1:]):
        w = hi - lo
        sizes.append((w, ((2, w, F), BF16), ((2 * w, F), BF16), 2 * (2 * w) * (2 * F) * F))
    square = ((2, F, F), BF16)
    opened = call(open_kernel, [size[2] for size in sizes], [vmem(), vmem()], [masks, src], 1 << 20)
    for tick in range(TICKS):
        final = tick == TICKS - 1
        order = [(c, side) for c in range(CHUNKS) for side in (0, 1)]
        if final and EAST_FIRST:
            order = [(c, side) for side in (0, 1) for c in range(CHUNKS)]
        pairs = list(opened)
        for c, side in order:
            w, trace, paired, flops = sizes[c]
            held = [table] if tick > TABLE else []
            if final and side:
                held.append(x_op)
            held_specs = [vmem()] * len(held) + [anywhere()]
            held.append(last)
            if side == 0:
                if tick == 0:
                    (last,) = call(
                        product_kernel, [trace], [vmem()] * 2 + held_specs, [pairs[c], x_op] + held, flops
                    )
                else:
                    body = functools.partial(east_kernel, tick, CUTS[c])
                    args = [masks, src, west[c], south[c], x_op] + held
                    specs = [vmem()] * 5 + held_specs
                    last, pairs[c] = call(body, [trace, paired], specs, args, flops)
                west[c] = swap(last, "bx", True) if final else shift(last, "bx", 1)
                if final:
                    ahead[c] = swap(last, "bx", False)
            else:
                (last,) = call(
                    product_kernel, [trace], [vmem()] * 2 + held_specs, [pairs[c], y_op] + held, flops
                )
                south[c] = swap(last, "by", True) if final else shift(last, "by", 1)
                if final:
                    above[c] = swap(last, "by", False)
        if tick == TABLE:
            (table,) = call(
                table_kernel, [square], [vmem(), vmem(), anywhere()], [coarse, fine, last], 1 << 27
            )
            last = table
    owned = SHOTS // nx
    spectra = []
    for c in range(CHUNKS):
        w, trace, paired, flops = sizes[c]
        (piece,) = call(
            mirror_kernel,
            [((w // owned, 2 * owned, F), BF16)],
            [vmem()] * 7 + [anywhere()],
            [masks, ahead[c], west[c], above[c], south[c], x_op, table, last],
            2 * flops,
            [pltpu.VMEM(paired[0], BF16), pltpu.VMEM(trace[0], BF16)],
        )
        spectra.append(piece)
        last = piece
    pieces = jnp.concatenate(spectra, axis=0)
    regrouped = lax.all_to_all(pieces, "bx", split_axis=0, concat_axis=0, tiled=True)
    weights, gain = line_weights(nx, owned)
    n = nx * 2 * owned
    (up,) = call(last_kernel, [((n, F), F32)], [vmem()] * 3, [weights, gain, regrouped.reshape(n, F)], 1 << 27)
    return up.reshape(1, owned, 2, nx, F)


def solution(mesh):
    placed = (
        P("bx", "by", None, None, None),
        P("bx", "by"),
        P("bx", "by", None, None, None),
        P("bx", "by", None, None, None),
    )

    return jax.shard_map(
        shards,
        mesh=mesh,
        in_specs=placed,
        out_specs=P("by", "bx", None, None, None),
        check_vma=False,
    )
```

```python
import functools

import jax
import jax.numpy as jnp
import numpy as np
from jax import lax
from jax.experimental import pallas as pl
from jax.experimental.pallas import tpu as pltpu
from jax.sharding import PartitionSpec as P


F = 1024
TICKS = 4
SHOTS = 128
CUTS = (0, 64, 128)
CHUNKS = len(CUTS) - 1
STEP = 512
TABLE = 1
EAST_FIRST = False
BF16 = jnp.bfloat16
F32 = jnp.float32
MIB = 1 << 20


def shift(value, axis, by):
    n = lax.axis_size(axis)
    return lax.ppermute(value, axis, [(i, (i + by) % n) for i in range(n)])


def swap(value, axis, odd):
    n = lax.axis_size(axis)
    partner = [k ^ 1 if not odd else min(max(((k + 1) ^ 1) - 1, 0), n - 1) for k in range(n)]
    partner = [k if partner[p] != k else p for k, p in enumerate(partner)]
    return lax.ppermute(value, axis, list(enumerate(partner)))


def vmem():
    return pl.BlockSpec(memory_space=pltpu.VMEM)


def anywhere():
    return pl.BlockSpec(memory_space=pl.ANY)


def call(kernel, outs, specs, args, flops, scratch=(), limit=12):
    return pl.pallas_call(
        kernel,
        out_shape=[jax.ShapeDtypeStruct(shape, kind) for shape, kind in outs],
        in_specs=specs,
        out_specs=[vmem() for _ in outs],
        scratch_shapes=list(scratch),
        compiler_params=pltpu.CompilerParams(vmem_limit_bytes=limit * MIB),
        cost_estimate=pl.CostEstimate(flops=flops, bytes_accessed=MIB, transcendentals=0),
    )(*args)


def combine(real, imag, out, lo, hi):
    w = out.shape[1]
    out[0, :, lo:hi] = (real[:w] - imag[w:]).astype(BF16)
    out[1, :, lo:hi] = (imag[:w] + real[w:]).astype(BF16)


def product(pair, operator, out):
    for c in range(0, F, STEP):
        real = jnp.dot(pair[...], operator[0, :, c : c + STEP], preferred_element_type=F32)
        imag = jnp.dot(pair[...], operator[1, :, c : c + STEP], preferred_element_type=F32)
        combine(real, imag, out, c, c + STEP)


def fill(pair, rows):
    w = pair.shape[0] // 2
    for part in range(2):
        for r in range(0, w, 16):
            pair[part * w + r : part * w + r + 16] = rows(part, r).astype(BF16)


FROM_WEST, FROM_SOUTH, FAR_X, FAR_Y, SIGN_X, _ = range(TICKS, TICKS + 6)


def row(masks, k):
    return masks[k : k + 1]


def open_kernel(masks, src, *pairs):
    for lo, pair in zip(CUTS, pairs):
        fill(pair, lambda c, r: row(masks, 0) * src[c, lo + r : lo + r + 16].astype(F32))


def east_kernel(tick, lo, masks, src, west, south, op, *rest):
    out, pair = rest[-2:]

    def rows(c, r):
        at = pl.ds(r, 16)
        return (
            row(masks, FROM_WEST) * west[c, at].astype(F32)
            + row(masks, FROM_SOUTH) * south[c, at].astype(F32)
            + row(masks, tick) * src[c, lo + r : lo + r + 16].astype(F32)
        )

    fill(pair, rows)
    product(pair, op, out)


def product_kernel(pair, op, *rest):
    product(pair, op, rest[-1])


def table_kernel(coarse, fine, _, out):
    for a in range(32):
        ca, sa = coarse[0, a : a + 1, :], coarse[1, a : a + 1, :]
        cb, sb = fine[0], fine[1]
        out[0, 32 * a : 32 * a + 32, :] = (ca * cb - sa * sb).astype(BF16)
        out[1, 32 * a : 32 * a + 32, :] = (sa * cb + ca * sb).astype(BF16)


def mirror_kernel(before, masks, east1, east2, north1, north2, op, table, held, out, pair, refl):
    if before:
        out[:before] = held[...]

    def rows(c, r):
        at = pl.ds(r, 16)
        along_x = east1[c, at].astype(F32) - row(masks, FAR_X) * east2[c, at].astype(F32)
        along_y = row(masks, FROM_SOUTH) * north2[c, at].astype(F32) - row(masks, FAR_Y) * north1[c, at].astype(F32)
        return row(masks, SIGN_X) * along_x + along_y

    fill(pair, rows)
    product(pair, op, refl)
    w = refl.shape[1]
    pair[:w] = refl[0]
    pair[w:] = refl[1]
    for c in range(0, F, STEP):
        cos = jnp.dot(pair[...], table[0, :, c : c + STEP], preferred_element_type=F32)
        sin = jnp.dot(pair[...], table[1, :, c : c + STEP], preferred_element_type=F32)
        combine(cos, -sin, refl, c, c + STEP)
    r = lax.broadcasted_iota(jnp.int32, (2 * w, 2 * w), 0)
    k = lax.broadcasted_iota(jnp.int32, (2 * w, 2 * w), 1)
    from_row = (r % 8) // 4 * w + r // 8 * 4 + r % 4
    pick = jnp.where(k == from_row, 1.0, 0.0).astype(BF16)
    for c in range(0, F, STEP):
        rows = jnp.concatenate([refl[0, :, c : c + STEP], refl[1, :, c : c + STEP]], axis=0)
        moved = jnp.dot(pick, rows, preferred_element_type=F32).astype(BF16)
        out[before:, :, c : c + STEP] = moved.reshape(w // 4, 8, STEP)


def last_kernel(weights, gain, got, out):
    out[...] = jnp.dot(weights[...], got[...], preferred_element_type=F32) * gain[...]


def line_parts():
    k = np.arange(F, dtype=np.int64)[None, :]
    a = np.arange(32, dtype=np.int64)[:, None]
    coarse = 2.0 * np.pi / F * (a * 32 * k % F)
    fine = 2.0 * np.pi / F * (a * k % F)
    pack = lambda t: jnp.asarray(np.stack([np.cos(t), np.sin(t)]).astype(np.float32))
    return pack(coarse), pack(fine)


def line_weights(blocks, owned):
    u = 2.0 * np.pi * (np.outer(np.arange(blocks), np.arange(blocks)) % blocks) / blocks
    cos = np.cos(u).astype(np.float32)
    sin = np.sin(u).astype(np.float32)
    w = np.zeros((owned, 2, blocks, blocks, 2, owned), np.float32)
    for s in range(owned):
        w[s, 0, :, :, 0, s] = cos.T
        w[s, 0, :, :, 1, s] = sin.T
        w[s, 1, :, :, 1, s] = cos.T
        w[s, 1, :, :, 0, s] = -sin.T
    m = np.where(np.arange(blocks) < blocks // 2, np.arange(blocks), np.arange(blocks) - blocks)
    g = 0.5 * (1.0 + m / np.sqrt(m * m + 1.0))
    n = owned * 2 * blocks
    gain = np.broadcast_to(g[None, None, :, None], (owned, 2, blocks, F)).reshape(n, F)[:, :1]
    return jnp.asarray(w.reshape(n, n), BF16), jnp.asarray(gain, F32)


def shards(source, start_tick, op_x, op_y):
    nx, ny = lax.axis_size("bx"), lax.axis_size("by")
    i, j = lax.axis_index("bx"), lax.axis_index("by")
    src, x_op, y_op = source[0, 0], op_x[0, 0], op_y[0, 0]
    first = start_tick[0, 0]
    flags = jnp.stack(
        [(first <= tick).astype(jnp.int32) for tick in range(TICKS)]
        + [
            (i > 0).astype(jnp.int32),
            (j > 0).astype(jnp.int32),
            ((i > 0) & (i < nx - 1)).astype(jnp.int32),
            (j < ny - 1).astype(jnp.int32),
            2 * (i & 1) - 1,
            2 * (j & 1) - 1,
        ]
        + [jnp.int32(0)] * 6
    )
    masks = jnp.broadcast_to(flags.astype(F32)[:, None], (16, F))
    coarse, fine = line_parts()
    west, south, ahead, above = ([None] * CHUNKS for _ in range(4))
    last = start_tick
    table = None
    sizes = []
    for lo, hi in zip(CUTS[:-1], CUTS[1:]):
        w = hi - lo
        sizes.append((w, ((2, w, F), BF16), ((2 * w, F), BF16), 2 * (2 * w) * (2 * F) * F))
    square = ((2, F, F), BF16)
    opened = call(open_kernel, [size[2] for size in sizes], [vmem(), vmem()], [masks, src], 1 << 20)
    for tick in range(TICKS):
        final = tick == TICKS - 1
        order = [(c, side) for c in range(CHUNKS) for side in (0, 1)]
        if final and EAST_FIRST:
            order = [(c, side) for side in (0, 1) for c in range(CHUNKS)]
        pairs = list(opened)
        for c, side in order:
            w, trace, paired, flops = sizes[c]
            held = [table] if tick > TABLE else []
            if final and side:
                held.append(x_op)
            held_specs = [vmem()] * len(held) + [anywhere()]
            held.append(last)
            if side == 0:
                if tick == 0:
                    (last,) = call(
                        product_kernel, [trace], [vmem()] * 2 + held_specs, [pairs[c], x_op] + held, flops
                    )
                else:
                    body = functools.partial(east_kernel, tick, CUTS[c])
                    args = [masks, src, west[c], south[c], x_op] + held
                    specs = [vmem()] * 5 + held_specs
                    last, pairs[c] = call(body, [trace, paired], specs, args, flops)
                west[c] = swap(last, "bx", True) if final else shift(last, "bx", 1)
                if final:
                    ahead[c] = swap(last, "bx", False)
            else:
                (last,) = call(
                    product_kernel, [trace], [vmem()] * 2 + held_specs, [pairs[c], y_op] + held, flops
                )
                south[c] = shift(last, "by", 1)
                if final:
                    above[c] = shift(last, "by", -1)
        if tick == TABLE:
            (table,) = call(
                table_kernel, [square], [vmem(), vmem(), anywhere()], [coarse, fine, last], 1 << 27
            )
            last = table
    owned = SHOTS // nx
    for c in range(CHUNKS):
        w, trace, paired, flops = sizes[c]
        before = CUTS[c] // owned
        (last,) = call(
            functools.partial(mirror_kernel, before),
            [((before + w // owned, 2 * owned, F), BF16)],
            [vmem()] * 7 + [vmem() if before else anywhere()],
            [masks, ahead[c], west[c], above[c], south[c], x_op, table, last],
            2 * flops,
            [pltpu.VMEM(paired[0], BF16), pltpu.VMEM(trace[0], BF16)],
        )
    pieces = last
    regrouped = lax.all_to_all(pieces, "bx", split_axis=0, concat_axis=0, tiled=True)
    weights, gain = line_weights(nx, owned)
    n = nx * 2 * owned
    (up,) = call(last_kernel, [((n, F), F32)], [vmem()] * 3, [weights, gain, regrouped.reshape(n, F)], 1 << 27)
    return up.reshape(1, owned, 2, nx, F)


def solution(mesh):
    placed = (
        P("bx", "by", None, None, None),
        P("bx", "by"),
        P("bx", "by", None, None, None),
        P("bx", "by", None, None, None),
    )

    return jax.shard_map(
        shards,
        mesh=mesh,
        in_specs=placed,
        out_specs=P("by", "bx", None, None, None),
        check_vma=False,
    )
```
